32 devices in a mesh: fsdp: 4 (over x, core), context: 4 (over z), tensor: 2 (over y).
Axes of the slice: x: 2, y: 2, z: 4, core: 2. Of those that a mesh axis runs over, the one named last changes fastest.
Arguments:
- block_input: float32 [8192, 768], P(('fsdp', 'context')), may hold values from -18 to 18
- ln1_gain: float32 [768], replicated, may hold values from 0.1 to 1.9
- ln1_shift: float32 [768], replicated, may hold values from -3 to 3
- qkv_weight: float32 [768, 3, 768], P(('fsdp', 'context'), None, 'tensor'), may hold values from -0.21875 to 0.21875
- qkv_bias: float32 [3, 768], P(None, 'tensor'), may hold values from -3 to 3
- feat_query: float32 [12, 64, 64], P('tensor'), may hold values from -1.5 to 1.5
- feat_key: float32 [12, 64, 64], P('tensor'), may hold values from -1.5 to 1.5
- out_weight: float32 [768, 768], P('tensor', ('fsdp', 'context')), may hold values from -3.5 to 3.5
- out_bias: float32 [768], replicated, may hold values from -3 to 3
- ln2_gain: float32 [768], replicated, may hold values from 0.1 to 1.9
- ln2_shift: float32 [768], replicated, may hold values from -3 to 3
- up_weight: float32 [768, 3072], P(('fsdp', 'context'), 'tensor'), may hold values from -0.21875 to 0.21875
- up_bias: float32 [3072], P('tensor'), may hold values from -3 to 3
- down_weight: float32 [3072, 768], P('tensor', ('fsdp', 'context')), may hold values from -0.109375 to 0.109375
- down_bias: float32 [768], replicated, may hold values from -3 to 3
- lengths: int32 [4], replicated, may hold values from 1024 to 2048, as said below
- deal: int32 [128], P(('fsdp', 'context')), may hold values from 0 to 127, as said below
- cotangent: float32 [8192, 768], P(('fsdp', 'context')), may hold values from -6 to 6
Outputs:
- dealt_output: float32 [128, 64, 768], P(('fsdp', 'context'), 'tensor')
- rms: float32 [3], replicated
- grad_input: float32 [8192, 768], P(('fsdp', 'context'))
- grad_ln1_gain: float32 [768], replicated
- grad_ln1_shift: float32 [768], replicated
- grad_qkv_weight: float32 [768, 3, 768], P(('fsdp', 'context'), None, 'tensor')
- grad_qkv_bias: float32 [3, 768], P(None, 'tensor')
- grad_feat_query: float32 [12, 64, 64], P('tensor')
- grad_feat_key: float32 [12, 64, 64], P('tensor')
- grad_out_weight: float32 [768, 768], P('tensor', ('fsdp', 'context'))
- grad_out_bias: float32 [768], replicated
- grad_ln2_gain: float32 [768], replicated
- grad_ln2_shift: float32 [768], replicated
- grad_up_weight: float32 [768, 3072], P(('fsdp', 'context'), 'tensor')
- grad_up_bias: float32 [3072], P('tensor')
- grad_down_weight: float32 [3072, 768], P('tensor', ('fsdp', 'context'))
- grad_down_bias: float32 [768], replicated
The draws below stay inside these ranges and needn't reach their ends.
Inputs may be any that keep to these rules, and one draw needn't show every extreme that they name: Sequence lengths; the 4 lengths sum to exactly 8160, and the last of them is exactly 2048. deal is a permutation of the 128 groups. Group j of the device with fsdp index f and context index e (groups numbered along fsdp, then context, then position) goes to position (f * 4 + d) * 8 + e * 2 + r, where the 8 groups of one device take every pair of d < 4 and r < 2 once.
All inputs are finite; a program needn't handle non-finite values.
Results may differ from the reference program's by a relative error of at most 0.0003.
Values sent between devices are 32-bit elements; how exact they have to be, the bound alone decides.
No kernel may reach another device: no remote copies, remote signals or barrier semaphores. Data moves between devices by JAX's collectives and lax.ppermute only.
A program may use at most 128 MiB of HBM per device.

```python
import jax
import jax.numpy as jnp
from jax import lax

D = 768
HEADS = 12
HD = 64
FF = 3072
GROUP = 64
SEQ_MIN = 1024
DATA_DEV = 16
TOKENS = 8192
SEQ_MAX = 2048
NSEQ = 4
NCHUNK = 128
CPD = 8
DEAL_SLOTS = 2


def draw_block_input(key, part):
    position = jnp.arange(TOKENS, dtype=jnp.float32)[:, None]
    factor = 1.0 + 2.0 * position / TOKENS
    base = jnp.clip(jax.random.normal(key, (TOKENS, D), jnp.float32), -6.0, 6.0)
    return base * factor


def draw_lengths(key, part):
    others = NSEQ - 1
    spare = TOKENS - GROUP // 2 - SEQ_MAX - others * SEQ_MIN
    limit = SEQ_MAX - SEQ_MIN
    base = spare // others
    remain = spare % others
    counting = jnp.arange(others, dtype=jnp.int32)
    extra = base + (counting < remain).astype(jnp.int32)
    reach = max(min(base, limit - base - 1), 0)
    pairs = others // 2
    moves = jax.random.randint(jax.random.fold_in(key, 11), (pairs,), 0, reach + 1, jnp.int32)
    signed = jnp.stack([moves, -moves], axis=1).reshape(2 * pairs)
    paired = jnp.concatenate([signed, jnp.zeros((others - 2 * pairs,), jnp.int32)])
    extra = extra + paired
    shuffle = jax.random.permutation(jax.random.fold_in(key, 12), others)
    leading = (SEQ_MIN + extra[shuffle]).astype(jnp.int32)
    return jnp.concatenate([leading, jnp.full((1,), SEQ_MAX, jnp.int32)]).astype(jnp.int32)


def draw_deal(key, part):
    peers = CPD // DEAL_SLOTS

    def one_device(device):
        shuffled = jax.random.permutation(jax.random.fold_in(key, device), CPD).astype(jnp.int32)
        fsdp_index = device // peers
        context_index = device % peers
        target = fsdp_index * peers + shuffled // DEAL_SLOTS
        return target * CPD + context_index * DEAL_SLOTS + shuffled % DEAL_SLOTS
    return jax.vmap(one_device)(jnp.arange(DATA_DEV, dtype=jnp.int32)).reshape(NCHUNK).astype(jnp.int32)


def shard_levels(key, extent, cuts, least, largest):
    def one(axis_at, parts):
        heights = jax.random.uniform(jax.random.fold_in(jax.random.fold_in(key, 6), axis_at), (parts,), jnp.float32, least / len(cuts), largest / len(cuts))
        return jnp.repeat(jnp.exp(heights), extent[axis_at] // parts).reshape((-1,) + (1,) * (len(extent) - axis_at - 1))

    factor_of = one(*cuts[0])
    for cut in cuts[1:]:
        factor_of = factor_of * one(*cut)
    return factor_of


def gaussian(own_key, dims, deviation, most, cuts=(), held_as=jnp.bfloat16):
    loudness = shard_levels(own_key, dims, cuts, -0.22, 0.18) if cuts else 1.0
    values = jax.random.normal(own_key, dims, jnp.float32) * deviation * loudness
    return jnp.minimum(jnp.maximum(values, -most), most).astype(held_as)


def setup_inputs(seed: int = 0) -> dict:
    arg_keys = jax.random.split(jax.random.key(seed), 19)
    block_input = draw_block_input(jax.random.fold_in(arg_keys[18], 71), 0)
    ln1_gain = jnp.clip(1.0 + 0.18 * jax.random.normal(arg_keys[1], (D,), jnp.float32), 0.1, 1.9)
    ln1_shift = gaussian(arg_keys[2], (D,), 0.5, 3.0, (), jnp.float32)
    qkv_weight = gaussian(arg_keys[3], (D, 3, D), D ** -0.5, 0.21875, ((0, 16), (2, 2)), jnp.float32)
    qkv_bias = gaussian(arg_keys[4], (3, D), 0.5, 3.0, ((1, 2),), jnp.float32)
    feat_query = gaussian(arg_keys[5], (HEADS, HD, HD), (HD // 4) ** -0.5, 1.5, ((0, 2),), jnp.float32)
    feat_key = gaussian(arg_keys[6], (HEADS, HD, HD), (HD // 4) ** -0.5, 1.5, ((0, 2),), jnp.float32)
    out_weight = gaussian(arg_keys[7], (D, D), (max(D // 256, 1)) ** -0.5, 3.5, ((0, 2), (1, 16)), jnp.float32)
    out_bias = gaussian(arg_keys[8], (D,), 0.5, 3.0, (), jnp.float32)
    ln2_gain = jnp.clip(1.0 + 0.18 * jax.random.normal(arg_keys[9], (D,), jnp.float32), 0.1, 1.9)
    ln2_shift = gaussian(arg_keys[10], (D,), 0.5, 3.0, (), jnp.float32)
    up_weight = gaussian(arg_keys[11], (D, FF), D ** -0.5, 0.21875, ((0, 16), (1, 2)), jnp.float32)
    up_bias = gaussian(arg_keys[12], (FF,), 0.5, 3.0, ((0, 2),), jnp.float32)
    down_weight = gaussian(arg_keys[13], (FF, D), FF ** -0.5, 0.109375, ((0, 2), (1, 16)), jnp.float32)
    down_bias = gaussian(arg_keys[14], (D,), 0.5, 3.0, (), jnp.float32)
    lengths = draw_lengths(jax.random.fold_in(arg_keys[18], 71), 0)
    deal = draw_deal(jax.random.fold_in(arg_keys[18], 71), 0)
    cotangent = gaussian(arg_keys[17], (TOKENS, D), 1.0, 6.0, ((0, 16),), jnp.float32)
    return {"block_input": block_input, "ln1_gain": ln1_gain, "ln1_shift": ln1_shift, "qkv_weight": qkv_weight, "qkv_bias": qkv_bias, "feat_query": feat_query, "feat_key": feat_key, "out_weight": out_weight, "out_bias": out_bias, "ln2_gain": ln2_gain, "ln2_shift": ln2_shift, "up_weight": up_weight, "up_bias": up_bias, "down_weight": down_weight, "down_bias": down_bias, "lengths": lengths, "deal": deal, "cotangent": cotangent}


HIGH = lax.Precision.HIGHEST
NORM_EPS = 1e-05

@jax.custom_vjp
def low(v):
    return lax.optimization_barrier(v.astype(jnp.bfloat16)).astype(jnp.float32)

@jax.custom_vjp
def low_back(v):
    return v

def low_keep(v):
    return (low(v), None)

def low_pass(kept, grad):
    return (grad,)

def back_keep(v):
    return (v, None)

def back_low(kept, grad):
    return (low(grad),)
low.defvjp(low_keep, low_pass)
low_back.defvjp(back_keep, back_low)

def layer_norm(values, gain, shift):
    middle = lax.optimization_barrier(jnp.mean(values, axis=-1, keepdims=True))
    centred = values - middle
    spread = lax.optimization_barrier(jnp.mean(centred * centred, axis=-1, keepdims=True))
    return centred * lax.rsqrt(spread + NORM_EPS) * gain + shift

def feature_map(heads, weight):
    logits = jnp.einsum('rhd,hde->rhe', heads, weight, precision=HIGH)
    return jnp.concatenate([jax.nn.softmax(logits, axis=-1), jax.nn.softmax(-logits, axis=-1)], axis=-1)

def reference(block_input, ln1_gain, ln1_shift, qkv_weight, qkv_bias, feat_query, feat_key, out_weight, out_bias, ln2_gain, ln2_shift, up_weight, up_bias, down_weight, down_bias, lengths, deal, cotangent):
    ends = jnp.cumsum(lengths).astype(jnp.int32)
    used = ends[-1]
    place = jnp.arange(TOKENS, dtype=jnp.int32)
    segment = lax.optimization_barrier(jnp.sum((ends[None, :] <= place[:, None]).astype(jnp.int32), axis=1)).astype(jnp.int32)
    valid = (place < used).astype(jnp.float32)
    block = min(512, TOKENS)
    blocks = TOKENS // block
    lower = jnp.arange(block)[:, None] >= jnp.arange(block)[None, :]

    def forward(block_input, ln1_gain, ln1_shift, qkv_weight, qkv_bias, feat_query, feat_key, out_weight, out_bias, ln2_gain, ln2_shift, up_weight, up_bias, down_weight, down_bias):

        def block_step(carry, pieces):
            state, normer, seg_carry = carry
            rows_in, seg_piece = pieces
            normed1 = layer_norm(rows_in, ln1_gain, ln1_shift)
            qkv = jnp.einsum('rd,dke->rke', normed1, qkv_weight, precision=HIGH) + qkv_bias
            queries = qkv[:, 0, :].reshape(block, HEADS, HD)
            keys = qkv[:, 1, :].reshape(block, HEADS, HD)
            values = qkv[:, 2, :].reshape(block, HEADS, HD)
            phi_q = feature_map(queries, feat_query)
            phi_k = feature_map(keys, feat_key)
            allowed = jnp.logical_and(lower, seg_piece[:, None] == seg_piece[None, :]).astype(jnp.float32)
            scores = jnp.einsum('ihf,jhf->hij', phi_q, phi_k, precision=HIGH) * allowed[None]
            numer = jnp.einsum('hij,jhd->ihd', scores, values, precision=HIGH)
            denom = jnp.einsum('hij->ih', scores)
            carried = (seg_piece == seg_carry).astype(jnp.float32)
            numer = numer + carried[:, None, None] * jnp.einsum('ihf,hfd->ihd', phi_q, state, precision=HIGH)
            denom = denom + carried[:, None] * jnp.einsum('ihf,hf->ih', phi_q, normer, precision=HIGH)
            attended = (numer / denom[:, :, None]).reshape(block, D)
            attn = jnp.dot(attended, out_weight, precision=HIGH) + out_bias
            hidden = rows_in + attn
            normed2 = layer_norm(hidden, ln2_gain, ln2_shift)
            active = jax.nn.gelu(jnp.dot(normed2, up_weight, precision=HIGH) + up_bias, approximate=True)
            mlp = jnp.dot(active, down_weight, precision=HIGH) + down_bias
            final_seg = seg_piece[-1]
            stays = (final_seg == seg_carry).astype(jnp.float32)
            tail_rows = (seg_piece == final_seg).astype(jnp.float32)[:, None, None]
            tail_k = phi_k * tail_rows
            state = stays * state + jnp.einsum('jhf,jhd->hfd', tail_k, values, precision=HIGH)
            normer = stays * normer + lax.optimization_barrier(jnp.sum(tail_k, axis=0))
            return ((state, normer, final_seg), (hidden + mlp, attn, mlp))
        start = (jnp.zeros((HEADS, 2 * HD, HD), jnp.float32), jnp.zeros((HEADS, 2 * HD), jnp.float32), jnp.array(-1, dtype=jnp.int32))
        pieces = (block_input.reshape(blocks, block, D), segment.reshape(blocks, block))
        _, (outs, attns, mlps) = lax.scan(jax.checkpoint(block_step), start, pieces)
        return (outs.reshape(TOKENS, D), (attns.reshape(TOKENS, D), mlps.reshape(TOKENS, D)))
    primals = (block_input, ln1_gain, ln1_shift, qkv_weight, qkv_bias, feat_query, feat_key, out_weight, out_bias, ln2_gain, ln2_shift, up_weight, up_bias, down_weight, down_bias)
    result, backward, branches = jax.vjp(forward, *primals, has_aux=True)
    attn, mlp = branches
    grad_y = cotangent.reshape(NCHUNK, GROUP, D)[deal].reshape(TOKENS, D) * valid[:, None]
    grads = backward(grad_y)
    order = jnp.zeros((NCHUNK,), jnp.int32).at[deal].set(jnp.arange(NCHUNK, dtype=jnp.int32))
    dealt_output = result.reshape(NCHUNK, GROUP, D)[order]
    weights = valid[:, None]
    squares = jnp.stack([jnp.sum(weights * result * result), jnp.sum(weights * attn * attn), jnp.sum(weights * mlp * mlp)])
    rms = jnp.sqrt(squares / (used.astype(jnp.float32) * D))
    return (dealt_output, rms, grads[0], grads[1], grads[2], grads[3], grads[4], grads[5], grads[6], grads[7], grads[8], grads[9], grads[10], grads[11], grads[12], grads[13], grads[14])
```

```python
import jax
import jax.numpy as jnp
from jax import lax
from jax.sharding import PartitionSpec as P

HIGH = lax.Precision.HIGH
FULL = lax.Precision.HIGHEST
NORM_EPS = 1e-05
DATA = ("fsdp", "context")
GELU_SCALE = 0.7978845608028654
GELU_CUBE = 0.044715


def dot(a, b, over, batch=((), ()), precision=HIGH):
    return lax.dot_general(
        a, b, (over, batch), precision=precision, preferred_element_type=jnp.float32
    )


def swap_with(axis, bit):
    count = lax.axis_size(axis)
    return [(i, i ^ bit) for i in range(count)]


def tensor_sum(part):
    count = lax.axis_size("tensor")
    bit = 1
    while bit < count:
        part = part + lax.ppermute(part, "tensor", swap_with("tensor", bit))
        bit *= 2
    return part


def data_sum(part):
    for axis in DATA:
        count = lax.axis_size(axis)
        bit = 1
        while bit < count:
            part = part + lax.ppermute(part, axis, swap_with(axis, bit))
            bit *= 2
    return part


def gather_rows(shard):
    return lax.all_gather(shard, DATA, axis=0, tiled=True)


def scatter_rows(whole):
    return lax.psum_scatter(whole, DATA, scatter_dimension=0, tiled=True)


def chain(state, normer, joins):
    heads, feats, head_dim = state.shape
    count = joins.shape[0]
    packed = jnp.concatenate([jnp.swapaxes(state, 1, 2), normer[:, None, :]], axis=1)
    lines = heads * (head_dim + 1)
    share = -(-lines // (8 * count)) * 8
    packed = jnp.pad(packed.reshape(lines, feats), ((0, share * count - lines), (0, 0)))
    slices = lax.all_to_all(
        packed.reshape(count, share, feats), DATA, split_axis=0, concat_axis=0, tiled=True
    )
    joined = dot(joins, slices.reshape(count, share * feats), ((1,), (0,)), precision=FULL)
    back = lax.all_to_all(
        joined.reshape(count, share, feats), DATA, split_axis=0, concat_axis=0, tiled=True
    )
    back = back.reshape(share * count, feats)[:lines].reshape(heads, head_dim + 1, feats)
    return back[:, :head_dim], back[:, head_dim]


def row_stats(values):
    middle = jnp.mean(values, axis=-1, keepdims=True)
    centred = values - middle
    spread = jnp.mean(centred * centred, axis=-1, keepdims=True)
    scale = lax.rsqrt(spread + NORM_EPS)
    return centred * scale, scale


def norm_backward(grad, hat, scale, gain):
    scaled = grad * gain
    return (
        scaled
        - jnp.mean(scaled, axis=-1, keepdims=True)
        - hat * jnp.mean(scaled * hat, axis=-1, keepdims=True)
    ) * scale


def body(
    block_input,
    ln1_gain,
    ln1_shift,
    qkv_weight,
    qkv_bias,
    feat_query,
    feat_key,
    out_weight,
    out_bias,
    ln2_gain,
    ln2_shift,
    up_weight,
    up_bias,
    down_weight,
    down_bias,
    lengths,
    deal,
    cotangent,
):
    rows, width = block_input.shape
    heads, head_dim = (feat_query.shape[0], feat_query.shape[1])
    local = heads * head_dim
    hidden_units = up_weight.shape[1]
    count = lax.axis_size(DATA)
    me = lax.axis_index(DATA)
    ends = jnp.cumsum(lengths)
    used = ends[-1]
    places = me * rows + jnp.arange(rows, dtype=jnp.int32)

    def segment_of(at):
        return jnp.sum((ends[None, :] <= at[:, None]).astype(jnp.int32), axis=1)

    segment = segment_of(places)
    starts = jnp.arange(count, dtype=jnp.int32) * rows
    firsts = segment_of(starts)
    finals = segment_of(starts + (rows - 1))
    order = jnp.arange(count)
    joins = jnp.logical_and(
        order[None, :] < order[:, None], finals[None, :] == firsts[:, None]
    ).astype(jnp.float32)
    from_first = (segment == segment[0]).astype(jnp.float32)
    to_final = (segment == segment[-1]).astype(jnp.float32)
    valid = (places < used).astype(jnp.float32)[:, None]
    lower = jnp.arange(rows)[:, None] >= jnp.arange(rows)[None, :]
    allowed = jnp.logical_and(lower, segment[:, None] == segment[None, :])

    first_pack = jnp.concatenate([qkv_weight.reshape(-1, 3 * local), out_weight.T], axis=1)
    second_pack = jnp.concatenate([up_weight, down_weight.T], axis=1)
    first_full = gather_rows(first_pack)
    second_full = gather_rows(second_pack)
    qkv_full = first_full[:, : 3 * local]
    out_full = first_full[:, 3 * local :]
    up_full = second_full[:, :hidden_units]
    down_full = second_full[:, hidden_units:]

    slots = deal.shape[0]
    group_rows = rows // slots
    tensor = lax.axis_size("tensor")
    part_rows = group_rows // tensor
    part_start = lax.axis_index("tensor") * part_rows
    per_peer = slots // lax.axis_size("context")
    slot_of = deal // slots % lax.axis_size("context") * per_peer + deal % per_peer
    counting = jnp.arange(slots, dtype=jnp.int32)
    source_of = jnp.sum(
        jnp.where(slot_of[None, :] == counting[:, None], counting[None, :], 0), axis=1
    )
    inbound = lax.all_to_all(
        cotangent.reshape(slots, group_rows, width),
        "context",
        split_axis=0,
        concat_axis=0,
        tiled=True,
    )

    hat1, scale1 = row_stats(block_input)
    normed1 = hat1 * ln1_gain + ln1_shift
    qkv = dot(normed1, qkv_full, ((1,), (0,))) + qkv_bias.reshape(1, 3 * local)
    split = qkv.reshape(rows, 3, heads, head_dim).transpose(1, 2, 0, 3)
    queries, keys, values = (split[0], split[1], split[2])

    def features(part, weight):
        logits = dot(part, weight, ((2,), (1,)), ((0,), (0,)))
        return jax.nn.softmax(logits, axis=-1), jax.nn.softmax(-logits, axis=-1)

    query_p, query_m = features(queries, feat_query)
    key_p, key_m = features(keys, feat_key)
    phi_q = jnp.concatenate([query_p, query_m], axis=-1)
    phi_k = jnp.concatenate([key_p, key_m], axis=-1)
    tail_k = phi_k * to_final[None, :, None]
    heads_b = ((0,), (0,))
    state_tail = dot(tail_k, values, ((1,), (1,)), heads_b)
    state_in, norm_in = chain(state_tail, jnp.sum(tail_k, axis=1), joins)
    scores = jnp.where(allowed[None], dot(phi_q, phi_k, ((2,), (2,)), heads_b), 0.0)
    head_q = phi_q * from_first[None, :, None]
    numer = dot(scores, values, ((2,), (1,)), heads_b) + dot(
        head_q, state_in, ((2,), (2,)), heads_b
    )
    denom = jnp.sum(scores, axis=2) + jnp.sum(head_q * norm_in[:, None, :], axis=2)
    attended = numer / denom[:, :, None]
    flat = attended.transpose(1, 0, 2).reshape(rows, local)
    attn = tensor_sum(dot(flat, out_full, ((1,), (1,)))) + out_bias
    hidden = block_input + attn

    hat2, scale2 = row_stats(hidden)
    normed2 = hat2 * ln2_gain + ln2_shift
    pre = dot(normed2, up_full, ((1,), (0,))) + up_bias
    bent = jnp.tanh(GELU_SCALE * (pre + GELU_CUBE * pre * pre * pre))
    active = 0.5 * pre * (1.0 + bent)
    slope = 0.5 * (1.0 + bent) + 0.5 * pre * (1.0 - bent * bent) * GELU_SCALE * (
        1.0 + 3.0 * GELU_CUBE * pre * pre
    )
    mlp_terms = dot(active, down_full, ((1,), (1,)))

    def own_part(array):
        return lax.dynamic_slice_in_dim(
            array.reshape(slots, group_rows, width), part_start, part_rows, 1
        )

    if tensor == 2:
        other = lax.dynamic_slice_in_dim(
            mlp_terms.reshape(slots, group_rows, width), part_rows - part_start, part_rows, 1
        )
        mlp_own = own_part(mlp_terms) + lax.ppermute(other, "tensor", [(0, 1), (1, 0)])
    else:
        mlp_own = own_part(tensor_sum(mlp_terms))
    mlp_own = mlp_own + down_bias
    attn_own = own_part(attn)
    result = own_part(hidden) + mlp_own
    outbound = jnp.take(result, source_of, axis=0)
    dealt_output = lax.all_to_all(outbound, "context", split_axis=0, concat_axis=0, tiled=True)
    weight_own = own_part(jnp.broadcast_to(valid, (rows, width)))[:, :, :1]
    squares = jnp.stack(
        [
            jnp.sum(weight_own * result * result),
            jnp.sum(weight_own * attn_own * attn_own),
            jnp.sum(weight_own * mlp_own * mlp_own),
        ]
    )

    grad_y = jnp.take(inbound, slot_of, axis=0).reshape(rows, width) * valid
    grad_pre = dot(grad_y, down_full, ((1,), (0,))) * slope
    grad_normed2 = tensor_sum(dot(grad_pre, up_full, ((1,), (1,))))
    second_grad = jnp.concatenate(
        [dot(normed2, grad_pre, ((0,), (0,))), dot(grad_y, active, ((0,), (0,)))], axis=1
    )
    second_own = scatter_rows(second_grad)
    grad_hidden = grad_y + norm_backward(grad_normed2, hat2, scale2, ln2_gain)

    out_grad = dot(grad_hidden, flat, ((0,), (0,)))
    grad_flat = dot(grad_hidden, out_full, ((1,), (0,)))
    grad_attended = grad_flat.reshape(rows, heads, head_dim).transpose(1, 0, 2)
    grad_numer = grad_attended / denom[:, :, None]
    grad_denom = -jnp.sum(grad_attended * attended, axis=2) / denom
    state_grad_in = dot(head_q, grad_numer, ((1,), (1,)), heads_b)
    norm_grad_in = jnp.sum(head_q * grad_denom[:, :, None], axis=1)
    state_grad, norm_grad = chain(state_grad_in, norm_grad_in, joins.T)
    pulls = jnp.where(
        allowed[None],
        dot(grad_numer, values, ((2,), (2,)), heads_b) + grad_denom[:, :, None],
        0.0,
    )
    grad_phi_q = dot(pulls, phi_k, ((2,), (1,)), heads_b) + from_first[None, :, None] * (
        dot(grad_numer, state_in, ((2,), (1,)), heads_b)
        + grad_denom[:, :, None] * norm_in[:, None, :]
    )
    grad_phi_k = dot(pulls, phi_q, ((1,), (1,)), heads_b) + to_final[None, :, None] * (
        dot(values, state_grad, ((2,), (1,)), heads_b) + norm_grad[:, None, :]
    )
    grad_values = dot(scores, grad_numer, ((1,), (1,)), heads_b) + dot(
        tail_k, state_grad, ((2,), (2,)), heads_b
    )

    def features_back(part, weight, plus, minus, grad):
        up, down = (grad[:, :, :head_dim], grad[:, :, head_dim:])
        grad_logits = plus * (up - jnp.sum(up * plus, axis=-1, keepdims=True)) - minus * (
            down - jnp.sum(down * minus, axis=-1, keepdims=True)
        )
        return (
            dot(grad_logits, weight, ((2,), (2,)), heads_b),
            dot(part, grad_logits, ((1,), (1,)), heads_b),
        )

    grad_queries, grad_feat_query = features_back(queries, feat_query, query_p, query_m, grad_phi_q)
    grad_keys, grad_feat_key = features_back(keys, feat_key, key_p, key_m, grad_phi_k)
    grad_qkv = (
        jnp.stack([grad_queries, grad_keys, grad_values])
        .transpose(2, 0, 1, 3)
        .reshape(rows, 3 * local)
    )
    grad_normed1_part = dot(grad_qkv, qkv_full, ((1,), (1,)))
    first_grad = jnp.concatenate([dot(normed1, grad_qkv, ((0,), (0,))), out_grad], axis=1)
    first_own = scatter_rows(first_grad)
    grad_normed1 = tensor_sum(grad_normed1_part)
    grad_input = grad_hidden + norm_backward(grad_normed1, hat1, scale1, ln1_gain)

    crossing = tensor_sum(
        jnp.concatenate(
            [
                jnp.sum(grad_normed1_part * hat1, axis=0),
                jnp.sum(grad_normed1_part, axis=0),
                jnp.pad(squares, (0, 125)),
            ]
        )
    )
    small = [
        grad_feat_query.reshape(-1),
        grad_feat_key.reshape(-1),
        jnp.sum(grad_qkv, axis=0),
        jnp.sum(grad_hidden, axis=0),
        jnp.sum(grad_normed2 * hat2, axis=0),
        jnp.sum(grad_normed2, axis=0),
        jnp.sum(grad_pre, axis=0),
        jnp.sum(grad_y, axis=0),
        crossing,
    ]
    joined = jnp.concatenate(small)
    joined = jnp.pad(joined, (0, -joined.shape[0] % 1024))
    total = data_sum(joined.reshape(-1, 128)).reshape(-1)
    pieces = []
    at = 0
    for part in small:
        pieces.append(total[at : at + part.shape[0]])
        at += part.shape[0]
    last = pieces[8]
    rms = jnp.sqrt(last[2 * width : 2 * width + 3] / (used.astype(jnp.float32) * width))
    return (
        dealt_output,
        rms,
        grad_input,
        last[:width],
        last[width : 2 * width],
        first_own[:, : 3 * local].reshape(-1, 3, local),
        pieces[2].reshape(3, local),
        pieces[0].reshape(feat_query.shape),
        pieces[1].reshape(feat_key.shape),
        first_own[:, 3 * local :].T,
        pieces[3],
        pieces[4],
        pieces[5],
        second_own[:, :hidden_units],
        pieces[6],
        second_own[:, hidden_units:].T,
        pieces[7],
    )


def solution(mesh):
    in_specs = (
        P(("fsdp", "context"), None),
        P(),
        P(),
        P(("fsdp", "context"), None, "tensor"),
        P(None, "tensor"),
        P("tensor", None, None),
        P("tensor", None, None),
        P("tensor", ("fsdp", "context")),
        P(),
        P(),
        P(),
        P(("fsdp", "context"), "tensor"),
        P("tensor"),
        P("tensor", ("fsdp", "context")),
        P(),
        P(),
        P(("fsdp", "context")),
        P(("fsdp", "context"), None),
    )
    out_specs = (
        P(("fsdp", "context"), "tensor", None),
        P(),
        P(("fsdp", "context"), None),
        P(),
        P(),
        P(("fsdp", "context"), None, "tensor"),
        P(None, "tensor"),
        P("tensor", None, None),
        P("tensor", None, None),
        P("tensor", ("fsdp", "context")),
        P(),
        P(),
        P(),
        P(("fsdp", "context"), "tensor"),
        P("tensor"),
        P("tensor", ("fsdp", "context")),
        P(),
    )
    return jax.shard_map(body, mesh=mesh, in_specs=in_specs, out_specs=out_specs, check_vma=False)
```

```python
import jax
import jax.numpy as jnp
from jax import lax
from jax.experimental import pallas as pl
from jax.experimental.pallas import tpu as pltpu
from jax.sharding import PartitionSpec as P

HIGH = lax.Precision.HIGH
FULL = lax.Precision.HIGHEST
NORM_EPS = 1e-05
DATA = ("fsdp", "context")
GELU_SCALE = 0.7978845608028654
GELU_CUBE = 0.044715


def dot(a, b, over, batch=((), ()), precision=HIGH):
    return lax.dot_general(
        a, b, (over, batch), precision=precision, preferred_element_type=jnp.float32
    )


def swap_with(axis, bit):
    count = lax.axis_size(axis)
    return [(i, i ^ bit) for i in range(count)]


def tensor_sum(part):
    count = lax.axis_size("tensor")
    bit = 1
    while bit < count:
        part = part + lax.ppermute(part, "tensor", swap_with("tensor", bit))
        bit *= 2
    return part


def data_sum(part):
    for axis in DATA:
        count = lax.axis_size(axis)
        bit = 1
        while bit < count:
            part = part + lax.ppermute(part, axis, swap_with(axis, bit))
            bit *= 2
    return part


def gather_rows(shard):
    return lax.all_gather(shard, DATA, axis=0, tiled=True)


def scatter_rows(whole):
    return lax.psum_scatter(whole, DATA, scatter_dimension=0, tiled=True)


def together(*values):
    return lax.optimization_barrier(values)


def small_grid():
    return lax.axis_size("fsdp") == 4 and lax.axis_size("context") == 4


def core_swap(part):
    return lax.ppermute(part, "fsdp", [(i, i ^ 1) for i in range(4)])


def side_swap(part):
    return lax.ppermute(part, "fsdp", [(i, i ^ 2) for i in range(4)])


def ring_next(part):
    return lax.ppermute(part, "context", [(i, (i + 1) % 4) for i in range(4)])


def put_in_order(parts, places):
    number = len(parts)
    rows, columns = parts[0].shape
    inside = pl.BlockSpec(memory_space=pltpu.VMEM)

    def kernel(at_ref, *refs):
        out_ref = refs[number]
        for i in range(number):
            start = pl.multiple_of(at_ref[i] * rows, 8)
            out_ref[pl.ds(start, rows), :] = refs[i][...]

    return pl.pallas_call(
        kernel,
        out_shape=jax.ShapeDtypeStruct((number * rows, columns), jnp.float32),
        in_specs=[pl.BlockSpec(memory_space=pltpu.SMEM)] + [inside] * number,
        out_specs=inside,
    )(places, *parts)


def gather_ring(shard):
    f, z = (lax.axis_index("fsdp"), lax.axis_index("context"))
    owns, sides, parts = ([shard], [], [])
    for k in range(4):
        new = [side_swap(owns[k])]
        if k < 3:
            new.append(ring_next(owns[k]))
        if k:
            new += [core_swap(owns[k - 1]), core_swap(sides[k - 1])]
        new = together(*new)
        sides.append(new[0])
        if k < 3:
            owns.append(new[1])
        parts += new[-2:] if k else []
    parts += [core_swap(owns[3]), core_swap(sides[3])]
    places = []
    for who in (f, f ^ 2):
        places += [who * 4 + (z - k) % 4 for k in range(4)]
    for k in range(4):
        places += [(who ^ 1) * 4 + (z - k) % 4 for who in (f, f ^ 2)]
    return put_in_order(owns + sides + parts, jnp.stack(places).astype(jnp.int32))


def take_at(array, index):
    return lax.dynamic_index_in_dim(array, index, 0, False)


def shift_down(array):
    z = lax.axis_index("context")
    total = take_at(array, z)
    for k in (1, 2, 3):
        pairs = [(i, (i + k) % 4) for i in range(4)]
        total = total + lax.ppermute(take_at(array, (z + k) % 4), "context", pairs)
    return total


def side_down(array, axis):
    x = lax.axis_index("fsdp") // 2
    got = side_swap(lax.dynamic_index_in_dim(array, 1 - x, axis, False))
    return lax.dynamic_index_in_dim(array, x, axis, False) + got


def scatter_steps(whole, small, gated, early):
    rows, columns = whole.shape
    most = columns // 384 * 256
    core = lax.axis_index("fsdp") % 2
    cut = whole.reshape(2, 2, 4, rows // 16, columns)
    got = core_swap(lax.dynamic_index_in_dim(cut, 1 - core, 1, False))
    held = lax.dynamic_index_in_dim(cut, core, 1, False) + got
    held, gated, early = together(held, gated, early)
    other = lax.ppermute(gated, "tensor", [(0, 1), (1, 0)])
    small = small + core_swap(small)
    first = side_down(held[..., :most], 0)
    second = shift_down(held[..., most:].transpose(1, 0, 2, 3))
    small = small + side_swap(small)
    first, second, small = together(first, second, small)
    small = small + lax.ppermute(small, "context", [(i, i ^ 1) for i in range(4)])
    own = [shift_down(first), side_down(second, 0)]
    small = small + lax.ppermute(small, "context", [(i, i ^ 2) for i in range(4)])
    own = jnp.concatenate(own, axis=-1)
    own, small, other = together(own, small, other)
    return own, small, gated + other, early


def reach_of(rows):
    longest = rows * lax.axis_size(DATA) // 4
    return -(-(longest - 1) // rows)


def chain(state, normer, joins, reach, reverse):
    heads, feats, head_dim = state.shape
    count = joins.shape[0]
    packed = jnp.concatenate([jnp.swapaxes(state, 1, 2), normer[:, None, :]], axis=1)
    if reach <= 4:
        me = lax.axis_index(DATA)
        weights = lax.dynamic_index_in_dim(joins, me, 0, keepdims=False)
        back = 0.0
        for step in range(1, reach + 1):
            pairs = [(i, i + step) for i in range(count - step)]
            if reverse:
                pairs = [(b, a) for a, b in pairs]
            at = me + step if reverse else me - step
            weight = lax.dynamic_index_in_dim(weights, jnp.clip(at, 0, count - 1), 0, False)
            back = back + weight * lax.ppermute(packed, DATA, pairs)
        return back[:, :head_dim], back[:, head_dim]
    lines = heads * (head_dim + 1)
    share = -(-lines // (8 * count)) * 8
    packed = jnp.pad(packed.reshape(lines, feats), ((0, share * count - lines), (0, 0)))
    slices = lax.all_to_all(
        packed.reshape(count, share, feats), DATA, split_axis=0, concat_axis=0, tiled=True
    )
    joined = dot(joins, slices.reshape(count, share * feats), ((1,), (0,)), precision=FULL)
    back = lax.all_to_all(
        joined.reshape(count, share, feats), DATA, split_axis=0, concat_axis=0, tiled=True
    )
    back = back.reshape(share * count, feats)[:lines].reshape(heads, head_dim + 1, feats)
    return back[:, :head_dim], back[:, head_dim]


def row_stats(values):
    middle = jnp.mean(values, axis=-1, keepdims=True)
    centred = values - middle
    spread = jnp.mean(centred * centred, axis=-1, keepdims=True)
    scale = lax.rsqrt(spread + NORM_EPS)
    return centred * scale, scale


def norm_backward(grad, hat, scale, gain):
    scaled = grad * gain
    return (
        scaled
        - jnp.mean(scaled, axis=-1, keepdims=True)
        - hat * jnp.mean(scaled * hat, axis=-1, keepdims=True)
    ) * scale


def body(
    block_input,
    ln1_gain,
    ln1_shift,
    qkv_weight,
    qkv_bias,
    feat_query,
    feat_key,
    out_weight,
    out_bias,
    ln2_gain,
    ln2_shift,
    up_weight,
    up_bias,
    down_weight,
    down_bias,
    lengths,
    deal,
    cotangent,
):
    rows, width = block_input.shape
    heads, head_dim = (feat_query.shape[0], feat_query.shape[1])
    local = heads * head_dim
    hidden_units = up_weight.shape[1]
    count = lax.axis_size(DATA)
    me = lax.axis_index(DATA)
    ends = jnp.cumsum(lengths)
    used = ends[-1]
    places = me * rows + jnp.arange(rows, dtype=jnp.int32)

    def segment_of(at):
        return jnp.sum((ends[None, :] <= at[:, None]).astype(jnp.int32), axis=1)

    segment = segment_of(places)
    starts = jnp.arange(count, dtype=jnp.int32) * rows
    firsts = segment_of(starts)
    finals = segment_of(starts + (rows - 1))
    order = jnp.arange(count)
    joins = jnp.logical_and(
        order[None, :] < order[:, None], finals[None, :] == firsts[:, None]
    ).astype(jnp.float32)
    from_first = (segment == segment[0]).astype(jnp.float32)
    to_final = (segment == segment[-1]).astype(jnp.float32)
    valid = (places < used).astype(jnp.float32)[:, None]
    lower = jnp.arange(rows)[:, None] >= jnp.arange(rows)[None, :]
    allowed = jnp.logical_and(lower, segment[:, None] == segment[None, :])

    first_shard = jnp.concatenate([qkv_weight.reshape(-1, 3 * local), out_weight.T], axis=1)
    second_shard = jnp.concatenate([up_weight, down_weight.T], axis=1)
    first_full = gather_ring(first_shard) if small_grid() else gather_rows(first_shard)
    first_full, second_shard = together(first_full, second_shard)
    second_full = gather_rows(second_shard)
    qkv_full, out_full = (first_full[:, : 3 * local], first_full[:, 3 * local :])
    up_full, down_full = (second_full[:, :hidden_units], second_full[:, hidden_units:])

    slots = deal.shape[0]
    group_rows = rows // slots
    tensor = lax.axis_size("tensor")
    part_rows = group_rows // tensor
    part_start = lax.axis_index("tensor") * part_rows
    per_peer = slots // lax.axis_size("context")
    slot_of = deal // slots % lax.axis_size("context") * per_peer + deal % per_peer
    counting = jnp.arange(slots, dtype=jnp.int32)
    source_of = jnp.sum(
        jnp.where(slot_of[None, :] == counting[:, None], counting[None, :], 0), axis=1
    )
    hat1, scale1 = row_stats(block_input)
    normed1 = hat1 * ln1_gain + ln1_shift
    qkv = dot(normed1, qkv_full, ((1,), (0,))) + qkv_bias.reshape(1, 3 * local)
    split = qkv.reshape(rows, 3, heads, head_dim).transpose(1, 2, 0, 3)
    queries, keys, values = (split[0], split[1], split[2])

    def features(part, weight):
        logits = dot(part, weight, ((2,), (1,)), ((0,), (0,)))
        return jax.nn.softmax(logits, axis=-1), jax.nn.softmax(-logits, axis=-1)

    query_p, query_m = features(queries, feat_query)
    key_p, key_m = features(keys, feat_key)
    phi_q = jnp.concatenate([query_p, query_m], axis=-1)
    phi_k = jnp.concatenate([key_p, key_m], axis=-1)
    tail_k = phi_k * to_final[None, :, None]
    heads_b = ((0,), (0,))
    state_tail = dot(tail_k, values, ((1,), (1,)), heads_b)
    state_in, norm_in = chain(
        state_tail, jnp.sum(tail_k, axis=1), joins, reach_of(rows), False
    )
    scores = jnp.where(allowed[None], dot(phi_q, phi_k, ((2,), (2,)), heads_b), 0.0)
    head_q = phi_q * from_first[None, :, None]
    state_in, norm_in, cotangent = together(state_in, norm_in, cotangent)
    inbound = lax.all_to_all(
        cotangent.reshape(slots, group_rows, width),
        "context",
        split_axis=0,
        concat_axis=0,
        tiled=True,
    )
    numer = dot(scores, values, ((2,), (1,)), heads_b) + dot(
        head_q, state_in, ((2,), (2,)), heads_b
    )
    denom = jnp.sum(scores, axis=2) + jnp.sum(head_q * norm_in[:, None, :], axis=2)
    attended = numer / denom[:, :, None]
    flat = attended.transpose(1, 0, 2).reshape(rows, local)
    attn_terms = dot(flat, out_full, ((1,), (1,)))
    attn = tensor_sum(attn_terms) + out_bias
    hidden = block_input + attn

    hat2, scale2 = row_stats(hidden)
    normed2 = hat2 * ln2_gain + ln2_shift
    pre = dot(normed2, up_full, ((1,), (0,))) + up_bias
    bent = jnp.tanh(GELU_SCALE * (pre + GELU_CUBE * pre * pre * pre))
    active = 0.5 * pre * (1.0 + bent)
    slope = 0.5 * (1.0 + bent) + 0.5 * pre * (1.0 - bent * bent) * GELU_SCALE * (
        1.0 + 3.0 * GELU_CUBE * pre * pre
    )
    mlp_terms = dot(active, down_full, ((1,), (1,)))

    grad_y = jnp.take(inbound, slot_of, axis=0).reshape(rows, width) * valid
    down_grad = dot(grad_y, active, ((0,), (0,)))
    grad_pre = dot(grad_y, down_full, ((1,), (0,))) * slope
    grad_normed2 = tensor_sum(dot(grad_pre, up_full, ((1,), (1,))))
    second_grad = jnp.concatenate([dot(normed2, grad_pre, ((0,), (0,))), down_grad], axis=1)
    second_own = scatter_rows(second_grad)
    grad_normed2 = grad_normed2 + 0.0 * second_grad[:1, :1]
    grad_hidden = grad_y + norm_backward(grad_normed2, hat2, scale2, ln2_gain)

    def own_part(array):
        return lax.dynamic_slice_in_dim(
            array.reshape(slots, group_rows, width), part_start, part_rows, 1
        )

    mlp_terms = mlp_terms + 0.0 * grad_normed2[:1, :1]
    if tensor == 2:
        other = lax.dynamic_slice_in_dim(
            mlp_terms.reshape(slots, group_rows, width), part_rows - part_start, part_rows, 1
        )
        mlp_own = own_part(mlp_terms) + lax.ppermute(other, "tensor", [(0, 1), (1, 0)])
    else:
        mlp_own = own_part(tensor_sum(mlp_terms))
    mlp_own = mlp_own + down_bias
    attn_own = own_part(attn)
    result = own_part(hidden) + mlp_own
    outbound = jnp.take(result, source_of, axis=0)
    weight_own = own_part(jnp.broadcast_to(valid, (rows, width)))[:, :, :1]
    squares = jnp.stack(
        [
            jnp.sum(weight_own * result * result),
            jnp.sum(weight_own * attn_own * attn_own),
            jnp.sum(weight_own * mlp_own * mlp_own),
        ]
    )

    out_grad = dot(grad_hidden, flat, ((0,), (0,)))
    grad_flat = dot(grad_hidden, out_full, ((1,), (0,)))
    grad_attended = grad_flat.reshape(rows, heads, head_dim).transpose(1, 0, 2)
    grad_numer = grad_attended / denom[:, :, None]
    grad_denom = -jnp.sum(grad_attended * attended, axis=2) / denom
    state_grad_in = dot(head_q, grad_numer, ((1,), (1,)), heads_b)
    norm_grad_in = jnp.sum(head_q * grad_denom[:, :, None], axis=1)
    state_grad, norm_grad = chain(
        state_grad_in, norm_grad_in, joins.T, reach_of(rows), True
    )
    state_grad, norm_grad, outbound = together(state_grad, norm_grad, outbound)
    dealt_output = lax.all_to_all(outbound, "context", split_axis=0, concat_axis=0, tiled=True)
    pulls = jnp.where(
        allowed[None],
        dot(grad_numer, values, ((2,), (2,)), heads_b) + grad_denom[:, :, None],
        0.0,
    )
    grad_phi_q = dot(pulls, phi_k, ((2,), (1,)), heads_b) + from_first[None, :, None] * (
        dot(grad_numer, state_in, ((2,), (1,)), heads_b)
        + grad_denom[:, :, None] * norm_in[:, None, :]
    )
    grad_phi_k = dot(pulls, phi_q, ((1,), (1,)), heads_b) + to_final[None, :, None] * (
        dot(values, state_grad, ((2,), (1,)), heads_b) + norm_grad[:, None, :]
    )
    grad_values = dot(scores, grad_numer, ((1,), (1,)), heads_b) + dot(
        tail_k, state_grad, ((2,), (2,)), heads_b
    )

    def features_back(part, weight, plus, minus, grad):
        up, down = (grad[:, :, :head_dim], grad[:, :, head_dim:])
        grad_logits = plus * (up - jnp.sum(up * plus, axis=-1, keepdims=True)) - minus * (
            down - jnp.sum(down * minus, axis=-1, keepdims=True)
        )
        return (
            dot(grad_logits, weight, ((2,), (2,)), heads_b),
            dot(part, grad_logits, ((1,), (1,)), heads_b),
        )

    grad_queries, grad_feat_query = features_back(queries, feat_query, query_p, query_m, grad_phi_q)
    grad_keys, grad_feat_key = features_back(keys, feat_key, key_p, key_m, grad_phi_k)
    grad_qkv = (
        jnp.stack([grad_queries, grad_keys, grad_values])
        .transpose(2, 0, 1, 3)
        .reshape(rows, 3 * local)
    )
    first_grad = jnp.concatenate([dot(normed1, grad_qkv, ((0,), (0,))), out_grad], axis=1)
    grad_normed1_part = dot(
        grad_qkv + 0.0 * first_grad[:1, :1], qkv_full, ((1,), (1,))
    )
    crossing = tensor_sum(
        jnp.concatenate(
            [
                jnp.sum(grad_normed1_part * hat1, axis=0),
                jnp.sum(grad_normed1_part, axis=0),
                jnp.pad(squares, (0, 125)),
            ]
        )
    )
    small = [
        grad_feat_query.reshape(-1),
        grad_feat_key.reshape(-1),
        jnp.sum(grad_qkv, axis=0),
        jnp.sum(grad_hidden, axis=0),
        jnp.sum(grad_normed2 * hat2, axis=0),
        jnp.sum(grad_normed2, axis=0),
        jnp.sum(grad_pre, axis=0),
        jnp.sum(grad_y, axis=0),
        crossing,
    ]
    joined = jnp.concatenate(small)
    joined = jnp.pad(joined, (0, -joined.shape[0] % 1024)).reshape(-1, 128)
    if small_grid() and tensor == 2:
        first_own, total, grad_normed1, dealt_output = scatter_steps(
            first_grad, joined, grad_normed1_part, dealt_output
        )
    else:
        first_own = scatter_rows(first_grad)
        total = data_sum(joined)
        grad_normed1 = tensor_sum(grad_normed1_part)
    total = total.reshape(-1)
    grad_input = grad_hidden + norm_backward(grad_normed1, hat1, scale1, ln1_gain)
    pieces = []
    at = 0
    for part in small:
        pieces.append(total[at : at + part.shape[0]])
        at += part.shape[0]
    last = pieces[8]
    rms = jnp.sqrt(last[2 * width : 2 * width + 3] / (used.astype(jnp.float32) * width))
    return (
        dealt_output,
        rms,
        grad_input,
        last[:width],
        last[width : 2 * width],
        first_own[:, : 3 * local].reshape(-1, 3, local),
        pieces[2].reshape(3, local),
        pieces[0].reshape(feat_query.shape),
        pieces[1].reshape(feat_key.shape),
        first_own[:, 3 * local :].T,
        pieces[3],
        pieces[4],
        pieces[5],
        second_own[:, :hidden_units],
        pieces[6],
        second_own[:, hidden_units:].T,
        pieces[7],
    )


def solution(mesh):
    in_specs = (
        P(("fsdp", "context"), None),
        P(),
        P(),
        P(("fsdp", "context"), None, "tensor"),
        P(None, "tensor"),
        P("tensor", None, None),
        P("tensor", None, None),
        P("tensor", ("fsdp", "context")),
        P(),
        P(),
        P(),
        P(("fsdp", "context"), "tensor"),
        P("tensor"),
        P("tensor", ("fsdp", "context")),
        P(),
        P(),
        P(("fsdp", "context")),
        P(("fsdp", "context"), None),
    )
    out_specs = (
        P(("fsdp", "context"), "tensor", None),
        P(),
        P(("fsdp", "context"), None),
        P(),
        P(),
        P(("fsdp", "context"), None, "tensor"),
        P(None, "tensor"),
        P("tensor", None, None),
        P("tensor", None, None),
        P("tensor", ("fsdp", "context")),
        P(),
        P(),
        P(),
        P(("fsdp", "context"), "tensor"),
        P("tensor"),
        P("tensor", ("fsdp", "context")),
        P(),
    )
    return jax.shard_map(body, mesh=mesh, in_specs=in_specs, out_specs=out_specs, check_vma=False)
```
